256 devices in a mesh: ctx: 32 (over x, y, core), head: 8 (over z).
Axes of the slice: x: 4, y: 4, z: 8, core: 2. Of those that a mesh axis runs over, the one named last changes fastest.
Arguments:
- queries: bfloat16 [8192, 8192], P('ctx', 'head'), may hold values from -110 to 110
- keys: bfloat16 [8192, 1024], P('ctx', 'head'), may hold values from -3.1 to 3.1
- values: bfloat16 [8192, 1024], P('ctx', 'head'), may hold values from -6 to 6
- cf_queries: bfloat16 [8192, 8192], P('ctx', 'head'), may hold values from -6 to 6
- cf_keys: bfloat16 [8192, 1024], P('ctx', 'head'), may hold values from -6 to 6
- cf_values: bfloat16 [8192, 1024], P('ctx', 'head'), may hold values from -6 to 6
- patch_source: int32 [8192], replicated, may hold values from -1 to 8191, as said below
- doc_lengths: int32 [32], replicated, may hold values from 1 to 4608, as said below
- out_weight: bfloat16 [8192, 4096], P('head'), may hold values from -0.5 to 0.5
Outputs:
- attn_out: bfloat16 [8192, 4096], P(('ctx', 'head'))
The draws below stay inside these ranges and needn't reach their ends.
Inputs may be any that keep to these rules, and one draw needn't show every extreme that they name: `patch_source`: exactly one aligned block of 128 positions of each index of ctx is replaced; its rows come from 16 different indices of ctx, 8 consecutive rows from each; no counterfactual position is used twice. `doc_lengths`: the lengths sum to 8192, and one document has exactly 4608 positions.
All inputs are finite; a program needn't handle non-finite values.
Results may differ from the reference program's by a relative error of at most 0.014.
Values may be sent and summed in bfloat16 or wider, within the bound.
A program may use at most 192 MiB of HBM per device.

```python
import math
import jax
import jax.numpy as jnp
from jax import lax

HEADS = 64
KV_HEADS = 8
HD = 128
DO = 4096
TOK_DEV = 256
BLK = 128
GROUPS = 16
CAP = 8
TOKENS = 8192
MOST = 4608
NDOCS = 32
N_CTX = 32


def layout(key):
    key_cuts = jax.random.fold_in(key, 11)
    key_place = jax.random.fold_in(key, 12)
    key_blocks = jax.random.fold_in(key, 13)
    key_sources = jax.random.fold_in(key, 14)
    key_local = jax.random.fold_in(key, 15)
    remainder = TOKENS - MOST
    cut_points = jnp.sort(jax.random.permutation(key_cuts, remainder - 1)[:NDOCS - 2] + 1).astype(jnp.int32)
    boundary = jnp.concatenate([jnp.zeros((1,), jnp.int32), cut_points, jnp.full((1,), remainder, jnp.int32)])
    short_lengths = boundary[1:] - boundary[:-1]
    long_index = jax.random.randint(key_place, (), 0, NDOCS)
    doc_index = jnp.arange(NDOCS, dtype=jnp.int32)
    from_short = jnp.clip(doc_index - (doc_index > long_index).astype(jnp.int32), 0, NDOCS - 2)
    lengths = jnp.where(doc_index == long_index, MOST, short_lengths[from_short]).astype(jnp.int32)
    block_count = TOK_DEV // BLK
    chosen = jax.random.randint(key_blocks, (N_CTX,), 0, block_count)
    source_devs = jax.vmap(lambda one_key: jax.random.permutation(one_key, N_CTX))(jax.random.split(key_sources, N_CTX))[:, :GROUPS]
    flat_sources = source_devs.reshape(-1).astype(jnp.int32)
    onehot = (flat_sources[:, None] == jnp.arange(N_CTX, dtype=jnp.int32)[None, :]).astype(jnp.int32)
    earlier = jnp.cumsum(onehot, axis=0) - onehot
    order = jnp.sum(earlier * onehot, axis=1)
    row_perm = jax.vmap(lambda one_key: jax.random.permutation(one_key, TOK_DEV))(jax.random.split(key_local, N_CTX)).astype(jnp.int32)
    local_rows = row_perm[flat_sources[:, None], order[:, None] * CAP + jnp.arange(CAP, dtype=jnp.int32)[None, :]]
    cf_pos = (flat_sources[:, None] * TOK_DEV + local_rows).reshape(N_CTX, BLK)
    base_pos = jnp.arange(N_CTX, dtype=jnp.int32)[:, None] * TOK_DEV + chosen[:, None] * BLK + jnp.arange(BLK, dtype=jnp.int32)[None, :]
    patch = jnp.full((TOKENS,), -1, jnp.int32).at[base_pos.reshape(-1)].set(cf_pos.reshape(-1))
    return (lengths, patch)


def base_keys(key):
    return jnp.clip(jax.random.normal(jax.random.fold_in(key, 31), (TOKENS, KV_HEADS * HD), jnp.float32), -3.0, 3.0)


def draw_patch_source(key, part):
    lengths, patch = layout(key)
    return patch


def draw_doc_lengths(key, part):
    lengths, patch = layout(key)
    return lengths


def draw_keys(key, part):
    raw = base_keys(key)
    return raw.astype(jnp.bfloat16)


def draw_queries(key, part):
    raw = jnp.clip(jax.random.normal(jax.random.fold_in(key, 41), (TOKENS, HEADS * HD), jnp.float32), -4.0, 4.0)
    return raw.astype(jnp.bfloat16)


def steps_of(key, dims, cuts, least, high):
    def one(dim, parts):
        heights = jax.random.uniform(jax.random.fold_in(jax.random.fold_in(key, 6), dim), (parts,), jnp.float32, least / len(cuts), high / len(cuts))
        return jnp.repeat(jnp.exp(heights), dims[dim] // parts).reshape((-1,) + (1,) * (len(dims) - dim - 1))

    gain = one(*cuts[0])
    for cut in cuts[1:]:
        gain = gain * one(*cut)
    return gain


def centred(own_key, extent, scale, bound, shards=(), held_as=jnp.bfloat16):
    gain = steps_of(own_key, extent, shards, -0.22, 0.18) if shards else 1.0
    values = jax.random.normal(own_key, extent, jnp.float32) * scale * gain
    return jnp.minimum(jnp.maximum(values, -bound), bound).astype(held_as)


def setup_inputs(seed: int = 0) -> dict:
    key_list = jax.random.split(jax.random.key(seed), 10)
    queries = draw_queries(jax.random.fold_in(key_list[9], 71), 0)
    keys = draw_keys(jax.random.fold_in(key_list[9], 71), 0)
    values = centred(key_list[2], (TOKENS, KV_HEADS * HD), 1.0, 6.0, ((0, 32), (1, 8)))
    cf_queries = centred(key_list[3], (TOKENS, HEADS * HD), 1.0, 6.0, ((0, 32), (1, 8)))
    cf_keys = centred(key_list[4], (TOKENS, KV_HEADS * HD), 1.0, 6.0, ((0, 32), (1, 8)))
    cf_values = centred(key_list[5], (TOKENS, KV_HEADS * HD), 1.0, 6.0, ((0, 32), (1, 8)))
    patch_source = draw_patch_source(jax.random.fold_in(key_list[9], 71), 0)
    doc_lengths = draw_doc_lengths(jax.random.fold_in(key_list[9], 71), 0)
    out_weight = centred(key_list[8], (HEADS * HD, DO), HD ** -0.5, 0.5, ((0, 8),))
    return {"queries": queries, "keys": keys, "values": values, "cf_queries": cf_queries, "cf_keys": cf_keys, "cf_values": cf_values, "patch_source": patch_source, "doc_lengths": doc_lengths, "out_weight": out_weight}


def reference(queries, keys, values, cf_queries, cf_keys, cf_values, patch_source, doc_lengths, out_weight):
    patched = patch_source >= 0
    source_rows = jnp.where(patched, patch_source, 0).astype(jnp.int32)
    query_rows = jnp.where(patched[:, None], cf_queries[source_rows], queries)
    key_rows = jnp.where(patched[:, None], cf_keys[source_rows], keys)
    value_rows = jnp.where(patched[:, None], cf_values[source_rows], values)
    positions = jnp.arange(TOKENS, dtype=jnp.int32)
    doc_ends = jnp.cumsum(doc_lengths).astype(jnp.int32)
    doc_of = lax.optimization_barrier(jnp.sum((positions[:, None] >= doc_ends[None, :]).astype(jnp.int32), axis=1))
    visible = (positions[:, None] >= positions[None, :]) & (doc_of[:, None] == doc_of[None, :])
    group_size = HEADS // KV_HEADS
    score_scale = 1.0 / math.sqrt(HD)

    def one_head(head):
        head_queries = lax.dynamic_slice_in_dim(query_rows, head * HD, HD, 1)
        kv_column = head // group_size * HD
        head_keys = lax.dynamic_slice_in_dim(key_rows, kv_column, HD, 1)
        head_values = lax.dynamic_slice_in_dim(value_rows, kv_column, HD, 1)
        scores = jnp.dot(head_queries, head_keys.T, preferred_element_type=jnp.float32) * score_scale
        scores = jnp.where(visible, scores, -jnp.inf)
        row_max = lax.optimization_barrier(jnp.max(scores, axis=1, keepdims=True))
        weights = jnp.exp(scores - row_max)
        row_sum = lax.optimization_barrier(jnp.sum(weights, axis=1, keepdims=True))
        mixed = jnp.dot(weights.astype(jnp.bfloat16), head_values, preferred_element_type=jnp.float32)
        return (mixed / row_sum).astype(jnp.bfloat16)
    per_head = lax.map(one_head, jnp.arange(HEADS, dtype=jnp.int32))
    attended = jnp.transpose(per_head, (1, 0, 2)).reshape(TOKENS, HEADS * HD)
    return jnp.dot(attended, out_weight, preferred_element_type=jnp.float32).astype(jnp.bfloat16)
```

```python
import math

import jax
import jax.numpy as jnp
from jax import lax
from jax.experimental import pallas as pl
from jax.experimental.pallas import tpu as pltpu
from jax.sharding import PartitionSpec as P

HD = 128
ROWS = 256
SLOT = 8
NEAR = 9
FAR = -(2.0**19)
EXP2 = math.log2(math.e) / math.sqrt(HD)
TILES = 8
MESH = pl.DeviceIdType.MESH
F32, BF16 = jnp.float32, jnp.bfloat16
VMEM = pl.BlockSpec(memory_space=pltpu.VMEM)
ANY = pl.BlockSpec(memory_space=pl.ANY)


def iota(shape, dim):
    return lax.broadcasted_iota(jnp.int32, shape, dim)


def dot(a, b):
    return jnp.dot(a, b, preferred_element_type=F32)


def patch_kernel(
    patch_ref, q_ref, k_ref, v_ref, cq_ref, ck_ref, cv_ref,
    oq_ref, okv_ref,
    send, recv, send_sem, recv_sem,
):
    n = patch_ref.shape[0]
    heads = cq_ref.shape[1] // HD
    wide = cq_ref.shape[1]
    me = lax.axis_index("ctx")
    barrier = pltpu.get_barrier_semaphore()

    def greet(i, carry):
        pl.semaphore_signal(
            barrier, inc=1, device_id={"ctx": lax.rem(me + i, n)}, device_id_type=MESH
        )
        return carry

    lax.fori_loop(1, n, greet, 0)

    table = patch_ref[...]
    mine = (table >> 8) == me
    ones = mine.astype(F32).astype(BF16)
    upto = (iota((ROWS, ROWS), 0) <= iota((ROWS, ROWS), 1)).astype(F32).astype(BF16)
    rank = jnp.where(mine, dot(ones, upto), 0.0).astype(BF16)
    row = jnp.where(mine, (table & (ROWS - 1)).astype(F32), 0.0).astype(BF16)
    spread = ((iota((n * SLOT, n), 0) >> 3) == iota((n * SLOT, n), 1)).astype(F32).astype(BF16)
    rank_all = dot(spread, rank)
    row_all = dot(spread, row)
    slot = ((iota((n * SLOT, ROWS), 0) & (SLOT - 1)) + 1).astype(F32)
    picked = jnp.sum(
        jnp.where(rank_all == slot, row_all + 1.0, 0.0), axis=1, keepdims=True
    ) - 1.0
    lane = iota((n * SLOT, ROWS), 1).astype(F32)
    choose = (lane == picked).astype(F32).astype(BF16)
    send[:, :, wide : wide + HD] = dot(choose, ck_ref[...]).reshape(n, SLOT, HD).astype(BF16)
    send[:, :, wide + HD :] = dot(choose, cv_ref[...]).reshape(n, SLOT, HD).astype(BF16)
    send[:, :, :wide] = dot(choose, cq_ref[...]).reshape(n, SLOT, wide).astype(BF16)
    pl.semaphore_wait(barrier, n - 1)

    def copy_to(i):
        peer = lax.rem(me + i, n)
        return pltpu.make_async_remote_copy(
            src_ref=send.at[peer],
            dst_ref=recv.at[me],
            send_sem=send_sem.at[i],
            recv_sem=recv_sem.at[i],
            device_id={"ctx": peer},
            device_id_type=MESH,
        )

    def copy_from(i):
        peer = lax.rem(me + n - i, n)
        return pltpu.make_async_remote_copy(
            src_ref=send.at[peer],
            dst_ref=recv.at[peer],
            send_sem=send_sem.at[i],
            recv_sem=recv_sem.at[i],
            device_id={"ctx": peer},
            device_id_type=MESH,
        )

    def start(i, carry):
        copy_to(i).start()
        return carry

    lax.fori_loop(1, n, start, 0)
    recv[me] = send[me]

    own = (patch_ref[pl.ds(me, 1), :] >> 8).astype(F32)
    same = iota((ROWS, ROWS), 0) == iota((ROWS, ROWS), 1)
    own_col = jnp.sum(jnp.where(same, own, 0.0), axis=1, keepdims=True)
    before = (own_col == own) & (iota((ROWS, ROWS), 1) < iota((ROWS, ROWS), 0))
    place = own_col * SLOT + jnp.sum(jnp.where(before, 1.0, 0.0), axis=1, keepdims=True)
    replaced = own_col >= 0.0
    lane = iota((ROWS, n * SLOT), 1).astype(F32)
    choose = ((lane == place) & replaced).astype(F32).astype(BF16)

    def arrive(i, carry):
        copy_from(i).wait_recv()
        return carry

    lax.fori_loop(1, n, arrive, 0)

    def merge(lo, base):
        got = recv[:, :, lo : lo + HD].astype(F32).reshape(n * SLOT, HD).astype(BF16)
        return jnp.where(replaced, dot(choose, got), base.astype(F32)).astype(BF16)

    okv_ref[0] = merge(wide, k_ref[...])
    okv_ref[1] = merge(wide + HD, v_ref[...])
    for h in range(heads):
        oq_ref[h] = merge(h * HD, q_ref[:, h * HD : (h + 1) * HD])

    def sent(i, carry):
        copy_to(i).wait_send()
        return carry

    lax.fori_loop(1, n, sent, 0)


def attend_kernel(
    lens_ref, q_ref, kv_ref,
    out_ref,
    kv, top, total, acc, send_sem, recv_sem, pass_sem, got_sem,
):
    heads = q_ref.shape[0]
    n = lax.axis_size("ctx")
    me = lax.axis_index("ctx")
    chip, core = me // 2, lax.rem(me, 2)
    other = 1 - core
    back = jnp.minimum(chip, NEAR)
    ahead = jnp.minimum(n // 2 - 1 - chip, NEAR)
    partner = {"ctx": chip * 2 + other}
    barrier = pltpu.get_barrier_semaphore()

    def greet(peer):
        pl.semaphore_signal(barrier, inc=1, device_id={"ctx": peer}, device_id_type=MESH)

    greet(chip * 2 + other)

    def greet_ahead(d, carry):
        greet(me + 2 * d)
        return carry

    def greet_back(d, carry):
        greet(me - 2 * d)
        return carry

    lax.fori_loop(1, ahead + 1, greet_ahead, 0)
    lax.fori_loop(1, back + 1, greet_back, 0)

    kv[0, core] = kv_ref[...]

    @pl.when(core == 0)
    def _():
        kv[0, 1] = jnp.zeros_like(kv_ref[...])

    lens = lens_ref[...].astype(F32)
    docs = lens.shape[1]
    d0, d1 = iota((docs, HD), 0), iota((docs, HD), 1)
    eye = iota((docs, docs), 0) == iota((docs, docs), 1)
    lens_col = jnp.sum(jnp.where(eye, lens, 0.0), axis=1, keepdims=True)
    ends = jnp.sum(jnp.where(d0 <= d1, lens_col, 0.0), axis=0, keepdims=True)
    starts = jnp.sum(jnp.where(d0 < d1, lens_col, 0.0), axis=0, keepdims=True)

    def in_doc(first, rows):
        pos = (first + iota((rows, HD), 0)).astype(F32)
        return (pos >= starts) & (pos < ends)

    far = jnp.where(in_doc(me * ROWS, ROWS), 0.0, FAR).astype(BF16)
    top[...] = jnp.full_like(top, -(2.0**22))
    total[...] = jnp.zeros_like(total)
    acc[...] = jnp.zeros_like(acc)

    pl.semaphore_wait(barrier, back + ahead + 1)

    def to_chip(d):
        return pltpu.make_async_remote_copy(
            src_ref=kv_ref,
            dst_ref=kv.at[d, core],
            send_sem=send_sem.at[d],
            recv_sem=recv_sem.at[d],
            device_id={"ctx": me + 2 * d},
            device_id_type=MESH,
        )

    def from_chip(d):
        return pltpu.make_async_remote_copy(
            src_ref=kv_ref,
            dst_ref=kv.at[d, core],
            send_sem=send_sem.at[d],
            recv_sem=recv_sem.at[d],
            device_id={"ctx": me - 2 * d},
            device_id_type=MESH,
        )

    def to_partner(d):
        return pltpu.make_async_remote_copy(
            src_ref=kv.at[d, core],
            dst_ref=kv.at[d, core],
            send_sem=pass_sem.at[d],
            recv_sem=got_sem.at[d],
            device_id=partner,
            device_id_type=MESH,
        )

    def from_partner(d):
        return pltpu.make_async_remote_copy(
            src_ref=kv.at[d, other],
            dst_ref=kv.at[d, other],
            send_sem=pass_sem.at[d],
            recv_sem=got_sem.at[d],
            device_id=partner,
            device_id_type=MESH,
        )

    own_to_partner = pltpu.make_async_remote_copy(
        src_ref=kv_ref,
        dst_ref=kv.at[0, core],
        send_sem=pass_sem.at[0],
        recv_sem=got_sem.at[0],
        device_id=partner,
        device_id_type=MESH,
    )

    @pl.when(core == 0)
    def _():
        own_to_partner.start()

    def send_out(d, carry):
        to_chip(d).start()
        return carry

    lax.fori_loop(1, ahead + 1, send_out, 0)

    def relay(d):
        from_chip(d).wait_recv()
        to_partner(d).start()

    @pl.when(back >= 1)
    def _():
        relay(1)

    @pl.when(core == 1)
    def _():
        from_partner(0).wait_recv()

    def unit(d, diagonal):
        keys = jnp.concatenate([kv[d, 0, 0], kv[d, 1, 0]], axis=0)
        vals = jnp.concatenate([kv[d, 0, 1], kv[d, 1, 1]], axis=0)
        span = 2 * ROWS
        first = (chip - d) * span
        marks = jnp.where(in_doc(first, span), 1.0, 0.0).astype(BF16)
        keys = jnp.concatenate([keys, marks], axis=1)
        vals = jnp.concatenate([vals, jnp.ones((span, HD), BF16)], axis=1)

        def head(h, carry):
            rows = jnp.concatenate([q_ref[h], far], axis=1)
            scores = lax.dot_general(
                rows, keys, (((1,), (1,)), ((), ())), preferred_element_type=F32
            )
            if diagonal:
                seen = first + iota((ROWS, span), 1) <= me * ROWS + iota((ROWS, span), 0)
                scores = jnp.where(seen, scores, 8.0 * FAR)
            old = top[h]
            new = jnp.maximum(old, jnp.max(scores, axis=1, keepdims=True))
            weights = jnp.concatenate(
                [
                    jnp.exp2((scores[:, t * HD : (t + 1) * HD] - new) * EXP2).astype(BF16)
                    for t in range(span // HD)
                ],
                axis=1,
            )
            scale = jnp.exp2((old - new) * EXP2)
            mixed = dot(weights, vals)
            top[h] = new
            acc[h] = acc[h] * scale + mixed[:, :HD]
            total[h] = total[h] * scale + mixed[:, HD:]
            return carry

        lax.fori_loop(0, heads, head, 0)

    unit(0, True)

    def step(d, carry):
        @pl.when(d < back)
        def _():
            relay(d + 1)

        from_partner(d).wait_recv()
        unit(d, False)
        return carry

    lax.fori_loop(1, back + 1, step, 0)

    for h in range(heads):
        out_ref[:, h * HD : (h + 1) * HD] = (acc[h] / total[h]).astype(BF16)

    def sent(d, carry):
        to_chip(d).wait_send()
        return carry

    def passed(d, carry):
        to_partner(d).wait_send()
        return carry

    lax.fori_loop(1, ahead + 1, sent, 0)
    lax.fori_loop(1, back + 1, passed, 0)

    @pl.when(core == 0)
    def _():
        own_to_partner.wait_send()


def project_kernel(
    a_ref, w_ref,
    out_ref,
    w, part, out_buf, in_buf, w_sem, send_sem, recv_sem,
):
    n = lax.axis_size("head")
    me = lax.axis_index("head")
    up, down = lax.rem(me + 1, n), lax.rem(me + n - 1, n)
    share = out_ref.shape[0]
    cols = out_ref.shape[1] // TILES
    barrier = pltpu.get_barrier_semaphore()
    for peer in (up, down):
        pl.semaphore_signal(barrier, inc=1, device_id={"head": peer}, device_id_type=MESH)

    def fetch(t):
        return pltpu.make_async_copy(
            w_ref.at[:, pl.ds(t * cols, cols)], w.at[t], w_sem.at[t]
        )

    for t in range(TILES):
        fetch(t).start()
    pl.semaphore_wait(barrier, 2)

    half = n // 2

    def hops(t):
        return (half, n - 1 - half) if t % 2 == 0 else (n - 1 - half, half)

    def move(t, way, s):
        slot = s if way == 0 else hops(t)[0] + s
        return pltpu.make_async_remote_copy(
            src_ref=out_buf.at[t, slot],
            dst_ref=in_buf.at[t, slot],
            send_sem=send_sem.at[t, slot],
            recv_sem=recv_sem.at[t, slot],
            device_id={"head": up if way == 0 else down},
            device_id_type=MESH,
        )

    def stage(t, s):
        if s == 0:
            fetch(t).wait()
            part[t] = dot(a_ref[...], w[t]).reshape(n, share, cols)
        total = part[t, me] if s == half else None
        for way in (0, 1):
            length = hops(t)[way]
            base = 0 if way == 0 else hops(t)[0]
            if s < length:
                left = length - s
                to = lax.rem(me + (left if way == 0 else n - left), n)
                value = part[t, to]
                if s > 0:
                    move(t, way, s - 1).wait_recv()
                    value = value + in_buf[t, base + s - 1].astype(F32)
                out_buf[t, base + s] = value.astype(BF16)
                move(t, way, s).start()
            if s == half:
                move(t, way, length - 1).wait_recv()
                total = total + in_buf[t, base + length - 1].astype(F32)
        if s == half:
            out_ref[:, t * cols : (t + 1) * cols] = total.astype(BF16)

    for r in range(TILES + half):
        for s in range(half + 1):
            if 0 <= r - s < TILES:
                stage(r - s, s)
    for t in range(TILES):
        for way in (0, 1):
            for s in range(hops(t)[way]):
                move(t, way, s).wait_send()


def per_device(
    queries, keys, values, cf_queries, cf_keys, cf_values, patch_source, doc_lengths, out_weight
):
    ctx = lax.axis_size("ctx")
    group = lax.axis_size("head")
    wide = queries.shape[1]
    heads = wide // HD
    dma = pltpu.SemaphoreType.DMA
    q, kv = pl.pallas_call(
        patch_kernel,
        name="patch",
        out_shape=(
            jax.ShapeDtypeStruct((heads, ROWS, HD), BF16),
            jax.ShapeDtypeStruct((2, ROWS, HD), BF16),
        ),
        in_specs=[VMEM] * 7,
        out_specs=(VMEM, VMEM),
        scratch_shapes=[
            pltpu.VMEM((ctx, SLOT, wide + 2 * HD), BF16),
            pltpu.VMEM((ctx, SLOT, wide + 2 * HD), BF16),
            dma((ctx,)),
            dma((ctx,)),
        ],
        compiler_params=pltpu.CompilerParams(collective_id=0, has_side_effects=True),
    )(
        patch_source.reshape(ctx, ROWS), queries, keys, values, cf_queries, cf_keys, cf_values
    )
    attended = pl.pallas_call(
        attend_kernel,
        name="attend",
        out_shape=jax.ShapeDtypeStruct((ROWS, wide), BF16),
        in_specs=[VMEM] * 3,
        out_specs=VMEM,
        scratch_shapes=[
            pltpu.VMEM((NEAR + 1, 2, 2, ROWS, HD), BF16),
            pltpu.VMEM((heads, ROWS, HD), F32),
            pltpu.VMEM((heads, ROWS, HD), F32),
            pltpu.VMEM((heads, ROWS, HD), F32),
            dma((NEAR + 1,)),
            dma((NEAR + 1,)),
            dma((NEAR + 1,)),
            dma((NEAR + 1,)),
        ],
        compiler_params=pltpu.CompilerParams(collective_id=1, has_side_effects=True),
    )(doc_lengths.reshape(1, -1), q, kv)
    feats = out_weight.shape[1]
    share, cols = ROWS // group, feats // TILES
    return pl.pallas_call(
        project_kernel,
        name="project",
        out_shape=jax.ShapeDtypeStruct((share, feats), BF16),
        in_specs=[VMEM, ANY],
        out_specs=VMEM,
        scratch_shapes=[
            pltpu.VMEM((TILES, wide, cols), BF16),
            pltpu.VMEM((TILES, group, share, cols), F32),
            pltpu.VMEM((TILES, group - 1, share, cols), BF16),
            pltpu.VMEM((TILES, group - 1, share, cols), BF16),
            dma((TILES,)),
            dma((TILES, group - 1)),
            dma((TILES, group - 1)),
        ],
        compiler_params=pltpu.CompilerParams(collective_id=2, has_side_effects=True),
    )(attended, out_weight)


def solution(mesh):
    in_specs = (
        P("ctx", "head"),
        P("ctx", "head"),
        P("ctx", "head"),
        P("ctx", "head"),
        P("ctx", "head"),
        P("ctx", "head"),
        P(),
        P(),
        P("head", None),
    )
    out_specs = P(("ctx", "head"), None)
    return jax.shard_map(
        per_device, mesh=mesh, in_specs=in_specs, out_specs=out_specs, check_vma=False
    )
```

```python
import math

import jax
import jax.numpy as jnp
from jax import lax
from jax.experimental import pallas as pl
from jax.experimental.pallas import tpu as pltpu
from jax.sharding import PartitionSpec as P

HD = 128
ROWS = 256
SLOT = 8
NEAR = 9
FAR = -(2.0**19)
EXP2 = math.log2(math.e) / math.sqrt(HD)
TILES = 8
MESH = pl.DeviceIdType.MESH
F32, BF16 = jnp.float32, jnp.bfloat16
VMEM = pl.BlockSpec(memory_space=pltpu.VMEM)
ANY = pl.BlockSpec(memory_space=pl.ANY)


def iota(shape, dim):
    return lax.broadcasted_iota(jnp.int32, shape, dim)


def dot(a, b):
    return jnp.dot(a, b, preferred_element_type=F32)


def patch_kernel(
    patch_ref, q_ref, k_ref, v_ref, cq_ref, ck_ref, cv_ref,
    oq_ref, okv_ref,
    send, recv, send_sem, recv_sem,
):
    n = patch_ref.shape[0]
    heads = cq_ref.shape[1] // HD
    wide = cq_ref.shape[1]
    me = lax.axis_index("ctx")
    barrier = pltpu.get_barrier_semaphore()

    def greet(i, carry):
        pl.semaphore_signal(
            barrier, inc=1, device_id={"ctx": lax.rem(me + i, n)}, device_id_type=MESH
        )
        return carry

    lax.fori_loop(1, n, greet, 0)

    table = patch_ref[...]
    mine = (table >> 8) == me
    ones = mine.astype(F32).astype(BF16)
    upto = (iota((ROWS, ROWS), 0) <= iota((ROWS, ROWS), 1)).astype(F32).astype(BF16)
    rank = jnp.where(mine, dot(ones, upto), 0.0).astype(BF16)
    row = jnp.where(mine, (table & (ROWS - 1)).astype(F32), 0.0).astype(BF16)
    spread = ((iota((n * SLOT, n), 0) >> 3) == iota((n * SLOT, n), 1)).astype(F32).astype(BF16)
    rank_all = dot(spread, rank)
    row_all = dot(spread, row)
    slot = ((iota((n * SLOT, ROWS), 0) & (SLOT - 1)) + 1).astype(F32)
    picked = jnp.sum(
        jnp.where(rank_all == slot, row_all + 1.0, 0.0), axis=1, keepdims=True
    ) - 1.0
    lane = iota((n * SLOT, ROWS), 1).astype(F32)
    choose = (lane == picked).astype(F32).astype(BF16)
    send[:, :, wide : wide + HD] = dot(choose, ck_ref[...]).reshape(n, SLOT, HD).astype(BF16)
    send[:, :, wide + HD :] = dot(choose, cv_ref[...]).reshape(n, SLOT, HD).astype(BF16)
    send[:, :, :wide] = dot(choose, cq_ref[...]).reshape(n, SLOT, wide).astype(BF16)
    pl.semaphore_wait(barrier, n - 1)

    def copy_to(i):
        peer = lax.rem(me + i, n)
        return pltpu.make_async_remote_copy(
            src_ref=send.at[peer],
            dst_ref=recv.at[me],
            send_sem=send_sem.at[i],
            recv_sem=recv_sem.at[i],
            device_id={"ctx": peer},
            device_id_type=MESH,
        )

    def copy_from(i):
        peer = lax.rem(me + n - i, n)
        return pltpu.make_async_remote_copy(
            src_ref=send.at[peer],
            dst_ref=recv.at[peer],
            send_sem=send_sem.at[i],
            recv_sem=recv_sem.at[i],
            device_id={"ctx": peer},
            device_id_type=MESH,
        )

    def start(i, carry):
        copy_to(i).start()
        return carry

    lax.fori_loop(1, n, start, 0)
    recv[me] = send[me]

    own = (patch_ref[pl.ds(me, 1), :] >> 8).astype(F32)
    same = iota((ROWS, ROWS), 0) == iota((ROWS, ROWS), 1)
    own_col = jnp.sum(jnp.where(same, own, 0.0), axis=1, keepdims=True)
    before = (own_col == own) & (iota((ROWS, ROWS), 1) < iota((ROWS, ROWS), 0))
    place = own_col * SLOT + jnp.sum(jnp.where(before, 1.0, 0.0), axis=1, keepdims=True)
    replaced = own_col >= 0.0
    lane = iota((ROWS, n * SLOT), 1).astype(F32)
    choose = ((lane == place) & replaced).astype(F32).astype(BF16)

    def arrive(i, carry):
        copy_from(i).wait_recv()
        return carry

    lax.fori_loop(1, n, arrive, 0)

    def merge(lo, base):
        got = recv[:, :, lo : lo + HD].astype(F32).reshape(n * SLOT, HD).astype(BF16)
        return jnp.where(replaced, dot(choose, got), base.astype(F32)).astype(BF16)

    okv_ref[0] = merge(wide, k_ref[...])
    okv_ref[1] = merge(wide + HD, v_ref[...])
    for h in range(heads):
        oq_ref[h] = merge(h * HD, q_ref[:, h * HD : (h + 1) * HD])

    def sent(i, carry):
        copy_to(i).wait_send()
        return carry

    lax.fori_loop(1, n, sent, 0)


def attend_kernel(
    lens_ref, q_ref, kv_ref,
    out_ref,
    rows, kv, top, total, acc, send_sem, recv_sem, pass_sem, got_sem,
):
    heads = q_ref.shape[0]
    n = lax.axis_size("ctx")
    me = lax.axis_index("ctx")
    chip, core = me // 2, lax.rem(me, 2)
    other = 1 - core
    back = jnp.minimum(chip, NEAR)
    ahead = jnp.minimum(n // 2 - 1 - chip, NEAR)
    partner = {"ctx": chip * 2 + other}
    barrier = pltpu.get_barrier_semaphore()

    def greet(peer):
        pl.semaphore_signal(barrier, inc=1, device_id={"ctx": peer}, device_id_type=MESH)

    greet(chip * 2 + other)

    def greet_ahead(d, carry):
        greet(me + 2 * d)
        return carry

    def greet_back(d, carry):
        greet(me - 2 * d)
        return carry

    lax.fori_loop(1, ahead + 1, greet_ahead, 0)
    lax.fori_loop(1, back + 1, greet_back, 0)

    kv[0, core, :, :, :HD] = kv_ref[...]

    @pl.when(core == 0)
    def _():
        kv[0, 1, :, :, :HD] = jnp.zeros_like(kv_ref[...])

    lens = lens_ref[...].astype(F32)
    docs = lens.shape[1]
    d0, d1 = iota((docs, HD), 0), iota((docs, HD), 1)
    eye = iota((docs, docs), 0) == iota((docs, docs), 1)
    lens_col = jnp.sum(jnp.where(eye, lens, 0.0), axis=1, keepdims=True)
    ends = jnp.sum(jnp.where(d0 <= d1, lens_col, 0.0), axis=0, keepdims=True)
    starts = jnp.sum(jnp.where(d0 < d1, lens_col, 0.0), axis=0, keepdims=True)

    def in_doc(first, rows):
        pos = (first + iota((rows, HD), 0)).astype(F32)
        return (pos >= starts) & (pos < ends)

    far = jnp.where(in_doc(me * ROWS, ROWS), 0.0, FAR).astype(BF16)
    for h in range(heads):
        rows[h, :, :HD] = q_ref[h]
        rows[h, :, HD:] = far

    def mark(d, carry):
        for c in (0, 1):
            here = in_doc(((chip - d) * 2 + c) * ROWS, ROWS)
            kv[d, c, 0, :, HD:] = jnp.where(here, 1.0, 0.0).astype(BF16)
            kv[d, c, 1, :, HD:] = jnp.ones((ROWS, HD), BF16)
        return carry

    lax.fori_loop(0, back + 1, mark, 0)

    pl.semaphore_wait(barrier, back + ahead + 1)

    def to_chip(d):
        return pltpu.make_async_remote_copy(
            src_ref=kv_ref,
            dst_ref=kv.at[d, core, :, :, pl.ds(0, HD)],
            send_sem=send_sem.at[d],
            recv_sem=recv_sem.at[d],
            device_id={"ctx": me + 2 * d},
            device_id_type=MESH,
        )

    def from_chip(d):
        return pltpu.make_async_remote_copy(
            src_ref=kv_ref,
            dst_ref=kv.at[d, core, :, :, pl.ds(0, HD)],
            send_sem=send_sem.at[d],
            recv_sem=recv_sem.at[d],
            device_id={"ctx": me - 2 * d},
            device_id_type=MESH,
        )

    def to_partner(d):
        return pltpu.make_async_remote_copy(
            src_ref=kv.at[d, core, :, :, pl.ds(0, HD)],
            dst_ref=kv.at[d, core, :, :, pl.ds(0, HD)],
            send_sem=pass_sem.at[d],
            recv_sem=got_sem.at[d],
            device_id=partner,
            device_id_type=MESH,
        )

    def from_partner(d):
        return pltpu.make_async_remote_copy(
            src_ref=kv.at[d, other, :, :, pl.ds(0, HD)],
            dst_ref=kv.at[d, other, :, :, pl.ds(0, HD)],
            send_sem=pass_sem.at[d],
            recv_sem=got_sem.at[d],
            device_id=partner,
            device_id_type=MESH,
        )

    own_to_partner = pltpu.make_async_remote_copy(
        src_ref=kv_ref,
        dst_ref=kv.at[0, core, :, :, pl.ds(0, HD)],
        send_sem=pass_sem.at[0],
        recv_sem=got_sem.at[0],
        device_id=partner,
        device_id_type=MESH,
    )

    @pl.when(core == 0)
    def _():
        own_to_partner.start()

    def send_out(d, carry):
        to_chip(d).start()
        return carry

    lax.fori_loop(1, ahead + 1, send_out, 0)

    def relay(d):
        from_chip(d).wait_recv()
        to_partner(d).start()

    @pl.when(back >= 1)
    def _():
        relay(1)

    @pl.when(core == 1)
    def _():
        from_partner(0).wait_recv()

    span = 2 * ROWS

    def unit(d, first):
        keys = kv[d, :, 0].reshape(span, 2 * HD)
        vals = kv[d, :, 1].reshape(span, 2 * HD)
        for h in range(heads):
            scores = lax.dot_general(
                rows[h], keys, (((1,), (1,)), ((), ())), preferred_element_type=F32
            )
            if first:
                seen = iota((ROWS, span), 1) <= core * ROWS + iota((ROWS, span), 0)
                scores = jnp.where(seen, scores, 8.0 * FAR)
            new = jnp.max(scores, axis=1, keepdims=True)
            if first:
                new = jnp.broadcast_to(new, (ROWS, HD))
            else:
                old = top[h]
                new = jnp.maximum(old, new)
                scale = jnp.exp2((old - new) * EXP2)
            weights = jnp.concatenate(
                [
                    jnp.exp2((scores[:, t * HD : (t + 1) * HD] - new) * EXP2).astype(BF16)
                    for t in range(span // HD)
                ],
                axis=1,
            )
            mixed = dot(weights, vals)
            top[h] = new
            if first:
                acc[h] = mixed[:, :HD]
                total[h] = mixed[:, HD:]
            else:
                acc[h] = acc[h] * scale + mixed[:, :HD]
                total[h] = total[h] * scale + mixed[:, HD:]

    unit(0, True)

    def step(d, carry):
        @pl.when(d < back)
        def _():
            relay(d + 1)

        from_partner(d).wait_recv()
        unit(d, False)
        return carry

    lax.fori_loop(1, back + 1, step, 0)

    for h in range(heads):
        out_ref[:, h * HD : (h + 1) * HD] = (acc[h] / total[h]).astype(BF16)

    def sent(d, carry):
        to_chip(d).wait_send()
        return carry

    def passed(d, carry):
        to_partner(d).wait_send()
        return carry

    lax.fori_loop(1, ahead + 1, sent, 0)
    lax.fori_loop(1, back + 1, passed, 0)

    @pl.when(core == 0)
    def _():
        own_to_partner.wait_send()


def project_kernel(
    a_ref, w_ref,
    out_ref,
    w, part, out_buf, in_buf, w_sem, send_sem, recv_sem,
):
    n = lax.axis_size("head")
    me = lax.axis_index("head")
    up, down = lax.rem(me + 1, n), lax.rem(me + n - 1, n)
    share = out_ref.shape[0]
    cols = out_ref.shape[1] // TILES
    barrier = pltpu.get_barrier_semaphore()
    for peer in (up, down):
        pl.semaphore_signal(barrier, inc=1, device_id={"head": peer}, device_id_type=MESH)

    def fetch(t):
        return pltpu.make_async_copy(
            w_ref.at[:, pl.ds(t * cols, cols)], w.at[t], w_sem.at[t]
        )

    for t in range(TILES):
        fetch(t).start()
    pl.semaphore_wait(barrier, 2)

    half = n // 2

    def hops(t):
        return (half, n - 1 - half) if t % 2 == 0 else (n - 1 - half, half)

    def move(t, way, s):
        slot = s if way == 0 else hops(t)[0] + s
        return pltpu.make_async_remote_copy(
            src_ref=out_buf.at[t, slot],
            dst_ref=in_buf.at[t, slot],
            send_sem=send_sem.at[t, slot],
            recv_sem=recv_sem.at[t, slot],
            device_id={"head": up if way == 0 else down},
            device_id_type=MESH,
        )

    def stage(t, s):
        if s == 0:
            fetch(t).wait()
            part[t] = dot(a_ref[...], w[t]).reshape(n, share, cols)
        total = part[t, me] if s == half else None
        for way in (0, 1):
            length = hops(t)[way]
            base = 0 if way == 0 else hops(t)[0]
            if s < length:
                left = length - s
                to = lax.rem(me + (left if way == 0 else n - left), n)
                value = part[t, to]
                if s > 0:
                    move(t, way, s - 1).wait_recv()
                    value = value + in_buf[t, base + s - 1].astype(F32)
                out_buf[t, base + s] = value.astype(BF16)
                move(t, way, s).start()
            if s == half:
                move(t, way, length - 1).wait_recv()
                total = total + in_buf[t, base + length - 1].astype(F32)
        if s == half:
            out_ref[:, t * cols : (t + 1) * cols] = total.astype(BF16)

    for r in range(TILES + half):
        for s in range(half + 1):
            if 0 <= r - s < TILES:
                stage(r - s, s)
    for t in range(TILES):
        for way in (0, 1):
            for s in range(hops(t)[way]):
                move(t, way, s).wait_send()


def per_device(
    queries, keys, values, cf_queries, cf_keys, cf_values, patch_source, doc_lengths, out_weight
):
    ctx = lax.axis_size("ctx")
    group = lax.axis_size("head")
    wide = queries.shape[1]
    heads = wide // HD
    dma = pltpu.SemaphoreType.DMA
    q, kv = pl.pallas_call(
        patch_kernel,
        name="patch",
        out_shape=(
            jax.ShapeDtypeStruct((heads, ROWS, HD), BF16),
            jax.ShapeDtypeStruct((2, ROWS, HD), BF16),
        ),
        in_specs=[VMEM] * 7,
        out_specs=(VMEM, VMEM),
        scratch_shapes=[
            pltpu.VMEM((ctx, SLOT, wide + 2 * HD), BF16),
            pltpu.VMEM((ctx, SLOT, wide + 2 * HD), BF16),
            dma((ctx,)),
            dma((ctx,)),
        ],
        compiler_params=pltpu.CompilerParams(collective_id=0, has_side_effects=True),
    )(
        patch_source.reshape(ctx, ROWS), queries, keys, values, cf_queries, cf_keys, cf_values
    )
    attended = pl.pallas_call(
        attend_kernel,
        name="attend",
        out_shape=jax.ShapeDtypeStruct((ROWS, wide), BF16),
        in_specs=[VMEM] * 3,
        out_specs=VMEM,
        scratch_shapes=[
            pltpu.VMEM((heads, ROWS, 2 * HD), BF16),
            pltpu.VMEM((NEAR + 1, 2, 2, ROWS, 2 * HD), BF16),
            pltpu.VMEM((heads, ROWS, HD), F32),
            pltpu.VMEM((heads, ROWS, HD), F32),
            pltpu.VMEM((heads, ROWS, HD), F32),
            dma((NEAR + 1,)),
            dma((NEAR + 1,)),
            dma((NEAR + 1,)),
            dma((NEAR + 1,)),
        ],
        compiler_params=pltpu.CompilerParams(collective_id=1, has_side_effects=True),
    )(doc_lengths.reshape(1, -1), q, kv)
    feats = out_weight.shape[1]
    share, cols = ROWS // group, feats // TILES
    return pl.pallas_call(
        project_kernel,
        name="project",
        out_shape=jax.ShapeDtypeStruct((share, feats), BF16),
        in_specs=[VMEM, ANY],
        out_specs=VMEM,
        scratch_shapes=[
            pltpu.VMEM((TILES, wide, cols), BF16),
            pltpu.VMEM((TILES, group, share, cols), F32),
            pltpu.VMEM((TILES, group - 1, share, cols), BF16),
            pltpu.VMEM((TILES, group - 1, share, cols), BF16),
            dma((TILES,)),
            dma((TILES, group - 1)),
            dma((TILES, group - 1)),
        ],
        compiler_params=pltpu.CompilerParams(collective_id=2, has_side_effects=True),
    )(attended, out_weight)


def solution(mesh):
    in_specs = (
        P("ctx", "head"),
        P("ctx", "head"),
        P("ctx", "head"),
        P("ctx", "head"),
        P("ctx", "head"),
        P("ctx", "head"),
        P(),
        P(),
        P("head", None),
    )
    out_specs = P(("ctx", "head"), None)
    return jax.shard_map(
        per_device, mesh=mesh, in_specs=in_specs, out_specs=out_specs, check_vma=False
    )
```

```python
import math

import jax
import jax.numpy as jnp
from jax import lax
from jax.experimental import pallas as pl
from jax.experimental.pallas import tpu as pltpu
from jax.sharding import PartitionSpec as P

HD = 128
ROWS = 256
SLOT = 8
SIDE = 4
FAR = -(2.0**19)
EXP2 = math.log2(math.e) / math.sqrt(HD)
TILES = 4
MESH = pl.DeviceIdType.MESH
F32, BF16 = jnp.float32, jnp.bfloat16
VMEM = pl.BlockSpec(memory_space=pltpu.VMEM)
ANY = pl.BlockSpec(memory_space=pl.ANY)


def iota(shape, dim):
    return lax.broadcasted_iota(jnp.int32, shape, dim)


def dot(a, b):
    return jnp.dot(a, b, preferred_element_type=F32)


def patch_kernel(
    patch_ref, q_ref, k_ref, v_ref, cq_ref, ck_ref, cv_ref,
    oq_ref, okv_ref,
    send, recv, send_sem, recv_sem,
):
    n = patch_ref.shape[0]
    heads = cq_ref.shape[1] // HD
    wide = cq_ref.shape[1]
    me = lax.axis_index("ctx")
    barrier = pltpu.get_barrier_semaphore()

    def greet(i, carry):
        pl.semaphore_signal(
            barrier, inc=1, device_id={"ctx": lax.rem(me + i, n)}, device_id_type=MESH
        )
        return carry

    lax.fori_loop(1, n, greet, 0)

    table = patch_ref[...]
    mine = (table >> 8) == me
    ones = mine.astype(F32).astype(BF16)
    upto = (iota((ROWS, ROWS), 0) <= iota((ROWS, ROWS), 1)).astype(F32).astype(BF16)
    rank = jnp.where(mine, dot(ones, upto), 0.0).astype(BF16)
    row = jnp.where(mine, (table & (ROWS - 1)).astype(F32), 0.0).astype(BF16)
    spread = ((iota((n * SLOT, n), 0) >> 3) == iota((n * SLOT, n), 1)).astype(F32).astype(BF16)
    rank_all = dot(spread, rank)
    row_all = dot(spread, row)
    slot = ((iota((n * SLOT, ROWS), 0) & (SLOT - 1)) + 1).astype(F32)
    picked = jnp.sum(
        jnp.where(rank_all == slot, row_all + 1.0, 0.0), axis=1, keepdims=True
    ) - 1.0
    lane = iota((n * SLOT, ROWS), 1).astype(F32)
    choose = (lane == picked).astype(F32).astype(BF16)
    send[:, :, wide : wide + HD] = dot(choose, ck_ref[...]).reshape(n, SLOT, HD).astype(BF16)
    send[:, :, wide + HD :] = dot(choose, cv_ref[...]).reshape(n, SLOT, HD).astype(BF16)
    send[:, :, :wide] = dot(choose, cq_ref[...]).reshape(n, SLOT, wide).astype(BF16)
    pl.semaphore_wait(barrier, n - 1)

    def copy_to(i):
        peer = lax.rem(me + i, n)
        return pltpu.make_async_remote_copy(
            src_ref=send.at[peer],
            dst_ref=recv.at[me],
            send_sem=send_sem.at[i],
            recv_sem=recv_sem.at[i],
            device_id={"ctx": peer},
            device_id_type=MESH,
        )

    def copy_from(i):
        peer = lax.rem(me + n - i, n)
        return pltpu.make_async_remote_copy(
            src_ref=send.at[peer],
            dst_ref=recv.at[peer],
            send_sem=send_sem.at[i],
            recv_sem=recv_sem.at[i],
            device_id={"ctx": peer},
            device_id_type=MESH,
        )

    def start(i, carry):
        copy_to(i).start()
        return carry

    lax.fori_loop(1, n, start, 0)
    recv[me] = send[me]

    own = (patch_ref[pl.ds(me, 1), :] >> 8).astype(F32)
    same = iota((ROWS, ROWS), 0) == iota((ROWS, ROWS), 1)
    own_col = jnp.sum(jnp.where(same, own, 0.0), axis=1, keepdims=True)
    before = (own_col == own) & (iota((ROWS, ROWS), 1) < iota((ROWS, ROWS), 0))
    place = own_col * SLOT + jnp.sum(jnp.where(before, 1.0, 0.0), axis=1, keepdims=True)
    replaced = own_col >= 0.0
    lane = iota((ROWS, n * SLOT), 1).astype(F32)
    choose = ((lane == place) & replaced).astype(F32).astype(BF16)

    def arrive(i, carry):
        copy_from(i).wait_recv()
        return carry

    lax.fori_loop(1, n, arrive, 0)

    def merge(lo, base):
        got = recv[:, :, lo : lo + HD].astype(F32).reshape(n * SLOT, HD).astype(BF16)
        return jnp.where(replaced, dot(choose, got), base.astype(F32)).astype(BF16)

    okv_ref[0] = merge(wide, k_ref[...])
    okv_ref[1] = merge(wide + HD, v_ref[...])
    for h in range(heads):
        oq_ref[h] = merge(h * HD, q_ref[:, h * HD : (h + 1) * HD])

    def sent(i, carry):
        copy_to(i).wait_send()
        return carry

    lax.fori_loop(1, n, sent, 0)


def attend_kernel(
    lens_ref, q_ref, kv_ref,
    out_ref,
    rows, kv, top, total, acc, send_sem, recv_sem, pass_sem, got_sem,
):
    heads = q_ref.shape[0]
    n = lax.axis_size("ctx")
    me = lax.axis_index("ctx")
    core = lax.rem(me, 2)
    chip = me // 2
    x, y = chip // SIDE, lax.rem(chip, SIDE)
    last = n // (2 * SIDE) - 1
    other = 1 - core
    way = 1 - 2 * core

    def device(to_x, to_y):
        return {"ctx": (to_x * SIDE + to_y) * 2 + core}

    def along(step):
        return lax.rem(y + SIDE + step, SIDE)

    partner = {"ctx": chip * 2 + other}
    barrier = pltpu.get_barrier_semaphore()

    def greet(to):
        pl.semaphore_signal(barrier, inc=1, device_id=to, device_id_type=MESH)

    corner_out = (x + 3 <= last) & (y == SIDE - 1)
    corner_in = (x >= 3) & (y == 0)
    greet(partner)
    greet(device(x, along(1)))
    greet(device(x, along(-1)))
    for cond, to in (
        (x < last, device(x + 1, y)),
        (x >= 1, device(x - 1, y)),
        (corner_out, device(x + 3, 0)),
        (corner_in, device(x - 3, SIDE - 1)),
    ):

        @pl.when(cond)
        def _(to=to):
            greet(to)

    lens = lens_ref[...].astype(F32)
    docs = lens.shape[1]
    d0, d1 = iota((docs, HD), 0), iota((docs, HD), 1)
    eye = iota((docs, docs), 0) == iota((docs, docs), 1)
    lens_col = jnp.sum(jnp.where(eye, lens, 0.0), axis=1, keepdims=True)
    ends = jnp.sum(jnp.where(d0 <= d1, lens_col, 0.0), axis=0, keepdims=True)
    starts = jnp.sum(jnp.where(d0 < d1, lens_col, 0.0), axis=0, keepdims=True)

    def in_doc(first):
        pos = (first + iota((ROWS, HD), 0)).astype(F32)
        return (pos >= starts) & (pos < ends)

    def as_int(cond):
        return jnp.where(cond, 1, 0)

    pl.semaphore_wait(
        barrier, 3 + as_int(x < last) + as_int(x >= 1) + as_int(corner_out) + as_int(corner_in)
    )

    def part(slot, c):
        return kv.at[slot, c, :, :, pl.ds(0, HD)]

    def remote(kind, src, slot, to):
        return pltpu.make_async_remote_copy(
            src_ref=src,
            dst_ref=part(slot, core),
            send_sem=send_sem.at[kind],
            recv_sem=recv_sem.at[kind],
            device_id=to,
            device_id_type=MESH,
        )

    def needs(dx, source, to):
        there = x >= dx
        near = jnp.where(dx == 0, to > source, True)
        far = jnp.where(dx == 2, source >= to - 1, True)
        corner = jnp.where(dx == 3, (to == 0) & (source == SIDE - 1), True)
        return there & near & far & corner

    def held(dx):
        return kv_ref if dx == 0 else part(dx * SIDE + y, core)

    def outgoing():
        yield 0, x < last, remote(0, kv_ref, SIDE + y, device(x + 1, y))
        yield 1, (x >= 1) & (x < last), remote(
            1, part(SIDE + y, core), 2 * SIDE + y, device(x + 1, y)
        )
        yield 2, corner_out, remote(2, kv_ref, 4 * SIDE - 1, device(x + 3, 0))
        for dx in range(3):
            yield 3 + dx, needs(dx, y, along(way)) | needs(dx, y, along(2)), remote(
                3 + dx, held(dx), dx * SIDE + y, device(x, along(way))
            )
            yield 6 + dx, needs(dx, y, along(-way)), remote(
                6 + dx, held(dx), dx * SIDE + y, device(x, along(-way))
            )
            slot = dx * SIDE + along(-way)
            yield 9 + dx, needs(dx, along(-way), along(way)), remote(
                9 + dx, part(slot, core), slot, device(x, along(way))
            )

    sends = {kind: (cond, copy) for kind, cond, copy in outgoing()}

    def arriving():
        yield 0, x >= 1, x >= 1, SIDE + y, device(x - 1, y)
        yield 1, x >= 2, x >= 2, 2 * SIDE + y, device(x - 1, y)
        yield 2, corner_in, corner_in, 4 * SIDE - 1, device(x - 3, SIDE - 1)
        for dx in range(3):
            source = along(-way)
            read = needs(dx, source, y)
            yield 3 + dx, read | needs(dx, source, along(way)), read, dx * SIDE + source, device(
                x, source
            )
            source = along(way)
            read = needs(dx, source, y)
            yield 6 + dx, read, read, dx * SIDE + source, device(x, source)
            source = along(2)
            read = needs(dx, source, y)
            yield 9 + dx, read, read, dx * SIDE + source, device(x, along(-way))

    arrivals = {kind: rest for kind, *rest in arriving()}

    def start(*kinds):
        for kind in kinds:
            cond, copy = sends[kind]

            @pl.when(cond)
            def _(copy=copy):
                copy.start()

    def relay(slot):
        return pltpu.make_async_remote_copy(
            src_ref=part(slot, core),
            dst_ref=part(slot, core),
            send_sem=pass_sem.at[slot],
            recv_sem=got_sem.at[slot],
            device_id=partner,
            device_id_type=MESH,
        )

    def relayed(slot):
        return pltpu.make_async_remote_copy(
            src_ref=part(slot, other),
            dst_ref=part(slot, other),
            send_sem=pass_sem.at[slot],
            recv_sem=got_sem.at[slot],
            device_id=partner,
            device_id_type=MESH,
        )

    def take(kind, *then):
        cond, read, slot, origin = arrivals[kind]

        @pl.when(cond)
        def _():
            remote(kind, kv_ref, slot, origin).wait_recv()

        start(*then)

        @pl.when(read)
        def _():
            relay(slot).start()

    own_to_partner = pltpu.make_async_remote_copy(
        src_ref=kv_ref,
        dst_ref=part(y, core),
        send_sem=pass_sem.at[y],
        recv_sem=got_sem.at[y],
        device_id=partner,
        device_id_type=MESH,
    )
    start(0, 3, 6, 2)

    @pl.when(core == 0)
    def _():
        own_to_partner.start()

    far = jnp.where(in_doc(me * ROWS), 0.0, FAR).astype(BF16)
    for h in range(heads):
        rows[h, :, :HD] = q_ref[h]
        rows[h, :, HD:] = far
    kv[y, core, :, :, :HD] = kv_ref[...]

    @pl.when(core == 0)
    def _():
        kv[y, 1, :, :, :HD] = jnp.zeros_like(kv_ref[...])

    def mark(slot):
        dx, source = slot // SIDE, lax.rem(slot, SIDE)
        for c in (0, 1):
            here = in_doc((((x - dx) * SIDE + source) * 2 + c) * ROWS)
            kv[slot, c, 0, :, HD:] = jnp.where(here, 1.0, 0.0).astype(BF16)
            kv[slot, c, 1, :, HD:] = jnp.ones((ROWS, HD), BF16)

    def mark_one(slot, carry):
        mark(slot)
        return carry

    lax.fori_loop(0, 3 * SIDE, mark_one, 0)
    mark(4 * SIDE - 1)

    @pl.when(core == 1)
    def _():
        relayed(y).wait_recv()

    span = 2 * ROWS

    def unit(slot, first):
        keys = kv[slot, :, 0].reshape(span, 2 * HD)
        vals = kv[slot, :, 1].reshape(span, 2 * HD)
        for h in range(heads):
            scores = lax.dot_general(
                rows[h], keys, (((1,), (1,)), ((), ())), preferred_element_type=F32
            )
            if first:
                seen = iota((ROWS, span), 1) <= core * ROWS + iota((ROWS, span), 0)
                scores = jnp.where(seen, scores, 8.0 * FAR)
            new = jnp.max(scores, axis=1, keepdims=True)
            if first:
                new = jnp.broadcast_to(new, (ROWS, HD))
            else:
                old = top[h]
                new = jnp.maximum(old, new)
                scale = jnp.exp2((old - new) * EXP2)
            weights = jnp.concatenate(
                [
                    jnp.exp2((scores[:, t * HD : (t + 1) * HD] - new) * EXP2).astype(BF16)
                    for t in range(span // HD)
                ],
                axis=1,
            )
            mixed = dot(weights, vals)
            top[h] = new
            if first:
                acc[h] = mixed[:, :HD]
                total[h] = mixed[:, HD:]
            else:
                acc[h] = acc[h] * scale + mixed[:, :HD]
                total[h] = total[h] * scale + mixed[:, HD:]

    unit(y, True)

    order = ((1, 0), (0, 1), (0, 3), (2, 0), (1, 1), (1, 3),
             (0, 2), (2, 1), (2, 3), (1, 2), (3, 3), (2, 2))
    code_x = sum(dx << (2 * i) for i, (dx, _) in enumerate(order))
    code_y = sum(dy << (2 * i) for i, (_, dy) in enumerate(order))

    def serve(i):
        if i == 0:
            take(0, 1, 4, 7)
            take(3, 9)
            take(6)
        if i == 3:
            take(1, 5, 8)
        if i == 4:
            take(4, 10)
            take(7)
            take(9)
        if i == 7:
            take(5, 11)
            take(8)
        if i == 9:
            take(10)
            take(2)
        if i == 11:
            take(11)

    def step(i, carry):
        for at in (0, 3, 4, 7, 9, 11):

            @pl.when(i == at)
            def _(at=at):
                serve(at)

        dx = (code_x >> (2 * i)) & 3
        source = lax.rem(y + ((code_y >> (2 * i)) & 3), SIDE)
        slot = dx * SIDE + source

        @pl.when(needs(dx, source, y))
        def _():
            relayed(slot).wait_recv()
            unit(slot, False)

        return carry

    lax.fori_loop(0, len(order), step, 0)

    for h in range(heads):
        out_ref[:, h * HD : (h + 1) * HD] = (acc[h] / total[h]).astype(BF16)

    for kind in range(12):
        cond, copy = sends[kind]

        @pl.when(cond)
        def _(copy=copy):
            copy.wait_send()

        _, read, slot, _ = arrivals[kind]

        @pl.when(read)
        def _(slot=slot):
            relay(slot).wait_send()

    @pl.when(core == 0)
    def _():
        own_to_partner.wait_send()


def project_kernel(
    a_ref, w_ref,
    out_ref,
    w, part, out_buf, in_buf, w_sem, send_sem, recv_sem,
):
    n = lax.axis_size("head")
    me = lax.axis_index("head")
    up, down = lax.rem(me + 1, n), lax.rem(me + n - 1, n)
    share = out_ref.shape[0]
    cols = out_ref.shape[1] // TILES
    barrier = pltpu.get_barrier_semaphore()
    for peer in (up, down):
        pl.semaphore_signal(barrier, inc=1, device_id={"head": peer}, device_id_type=MESH)

    def fetch(t):
        return pltpu.make_async_copy(
            w_ref.at[:, pl.ds(t * cols, cols)], w.at[t], w_sem.at[t]
        )

    for t in range(TILES):
        fetch(t).start()
    pl.semaphore_wait(barrier, 2)

    half = n // 2

    def hops(t):
        return (half, n - 1 - half) if t % 2 == 0 else (n - 1 - half, half)

    def move(t, way, s):
        slot = s if way == 0 else hops(t)[0] + s
        return pltpu.make_async_remote_copy(
            src_ref=out_buf.at[t, slot],
            dst_ref=in_buf.at[t, slot],
            send_sem=send_sem.at[t, slot],
            recv_sem=recv_sem.at[t, slot],
            device_id={"head": up if way == 0 else down},
            device_id_type=MESH,
        )

    def stage(t, s):
        if s == 0:
            fetch(t).wait()
            part[t] = dot(a_ref[...], w[t]).reshape(n, share, cols)
        total = part[t, me] if s == half else None
        for way in (0, 1):
            length = hops(t)[way]
            base = 0 if way == 0 else hops(t)[0]
            if s < length:
                left = length - s
                to = lax.rem(me + (left if way == 0 else n - left), n)
                value = part[t, to]
                if s > 0:
                    move(t, way, s - 1).wait_recv()
                    value = value + in_buf[t, base + s - 1].astype(F32)
                out_buf[t, base + s] = value.astype(BF16)
                move(t, way, s).start()
            if s == half:
                move(t, way, length - 1).wait_recv()
                total = total + in_buf[t, base + length - 1].astype(F32)
        if s == half:
            out_ref[:, t * cols : (t + 1) * cols] = total.astype(BF16)

    for s in range(half + 1):
        for t in range(TILES):
            stage(t, s)
    for t in range(TILES):
        for way in (0, 1):
            for s in range(hops(t)[way]):
                move(t, way, s).wait_send()


def per_device(
    queries, keys, values, cf_queries, cf_keys, cf_values, patch_source, doc_lengths, out_weight
):
    ctx = lax.axis_size("ctx")
    group = lax.axis_size("head")
    wide = queries.shape[1]
    heads = wide // HD
    dma = pltpu.SemaphoreType.DMA
    q, kv = pl.pallas_call(
        patch_kernel,
        name="patch",
        out_shape=(
            jax.ShapeDtypeStruct((heads, ROWS, HD), BF16),
            jax.ShapeDtypeStruct((2, ROWS, HD), BF16),
        ),
        in_specs=[VMEM] * 7,
        out_specs=(VMEM, VMEM),
        scratch_shapes=[
            pltpu.VMEM((ctx, SLOT, wide + 2 * HD), BF16),
            pltpu.VMEM((ctx, SLOT, wide + 2 * HD), BF16),
            dma((ctx,)),
            dma((ctx,)),
        ],
        compiler_params=pltpu.CompilerParams(collective_id=0, has_side_effects=True),
    )(
        patch_source.reshape(ctx, ROWS), queries, keys, values, cf_queries, cf_keys, cf_values
    )
    attended = pl.pallas_call(
        attend_kernel,
        name="attend",
        out_shape=jax.ShapeDtypeStruct((ROWS, wide), BF16),
        in_specs=[VMEM] * 3,
        out_specs=VMEM,
        scratch_shapes=[
            pltpu.VMEM((heads, ROWS, 2 * HD), BF16),
            pltpu.VMEM((4 * SIDE, 2, 2, ROWS, 2 * HD), BF16),
            pltpu.VMEM((heads, ROWS, HD), F32),
            pltpu.VMEM((heads, ROWS, HD), F32),
            pltpu.VMEM((heads, ROWS, HD), F32),
            dma((12,)),
            dma((12,)),
            dma((4 * SIDE,)),
            dma((4 * SIDE,)),
        ],
        compiler_params=pltpu.CompilerParams(collective_id=1, has_side_effects=True),
    )(doc_lengths.reshape(1, -1), q, kv)
    feats = out_weight.shape[1]
    share, cols = ROWS // group, feats // TILES
    return pl.pallas_call(
        project_kernel,
        name="project",
        out_shape=jax.ShapeDtypeStruct((share, feats), BF16),
        in_specs=[VMEM, ANY],
        out_specs=VMEM,
        scratch_shapes=[
            pltpu.VMEM((TILES, wide, cols), BF16),
            pltpu.VMEM((TILES, group, share, cols), F32),
            pltpu.VMEM((TILES, group - 1, share, cols), BF16),
            pltpu.VMEM((TILES, group - 1, share, cols), BF16),
            dma((TILES,)),
            dma((TILES, group - 1)),
            dma((TILES, group - 1)),
        ],
        compiler_params=pltpu.CompilerParams(collective_id=2, has_side_effects=True),
    )(attended, out_weight)


def solution(mesh):
    in_specs = (
        P("ctx", "head"),
        P("ctx", "head"),
        P("ctx", "head"),
        P("ctx", "head"),
        P("ctx", "head"),
        P("ctx", "head"),
        P(),
        P(),
        P("head", None),
    )
    out_specs = P(("ctx", "head"), None)
    return jax.shard_map(
        per_device, mesh=mesh, in_specs=in_specs, out_specs=out_specs, check_vma=False
    )
```

```python
import math

import jax
import jax.numpy as jnp
from jax import lax
from jax.experimental import pallas as pl
from jax.experimental.pallas import tpu as pltpu
from jax.sharding import PartitionSpec as P

HD = 128
ROWS = 256
BLK = 128
SLOT = 8
SIDE = 4
FAR = -(2.0**19)
EXP2 = math.log2(math.e) / math.sqrt(HD)
TILES = 4
MESH = pl.DeviceIdType.MESH
F32, BF16 = jnp.float32, jnp.bfloat16
VMEM = pl.BlockSpec(memory_space=pltpu.VMEM)
ANY = pl.BlockSpec(memory_space=pl.ANY)


def iota(shape, dim):
    return lax.broadcasted_iota(jnp.int32, shape, dim)


def dot(a, b):
    return jnp.dot(a, b, preferred_element_type=F32)


def layer_kernel(
    patch_ref, lens_ref, q_ref, k_ref, v_ref, cq_ref, ck_ref, cv_ref, w_ref,
    out_ref,
    give_kv, take_kv, give_q, take_q, own, rows, kv, top, total, acc, mixed_heads,
    w, part_sum, out_buf, in_buf,
    give_kv_sem, take_kv_sem, give_q_sem, take_q_sem,
    send_sem, recv_sem, pass_sem, got_sem, w_sem, up_sem, down_sem,
):
    wide = cq_ref.shape[1]
    heads = wide // HD
    n = lax.axis_size("ctx")
    me = lax.axis_index("ctx")
    core = lax.rem(me, 2)
    chip = me // 2
    x, y = chip // SIDE, lax.rem(chip, SIDE)
    last = n // (2 * SIDE) - 1
    other = 1 - core
    way = 1 - 2 * core
    groups = lax.axis_size("head")
    group = lax.axis_index("head")
    up, down = lax.rem(group + 1, groups), lax.rem(group + groups - 1, groups)
    share = out_ref.shape[0]
    cols = out_ref.shape[1] // TILES

    barrier = pltpu.get_barrier_semaphore()

    def greet(i, carry):
        pl.semaphore_signal(
            barrier, inc=1, device_id={"ctx": lax.rem(me + i, n)}, device_id_type=MESH
        )
        return carry

    lax.fori_loop(1, n, greet, 0)
    for peer in (up, down):
        pl.semaphore_signal(barrier, inc=1, device_id={"head": peer}, device_id_type=MESH)

    def fetch(t):
        return pltpu.make_async_copy(
            w_ref.at[:, pl.ds(t * cols, cols)], w.at[t], w_sem.at[t]
        )

    for t in range(TILES):
        fetch(t).start()

    table = patch_ref[...]
    mine = (table >> 8) == me
    ones = mine.astype(F32).astype(BF16)
    upto = (iota((BLK, BLK), 0) <= iota((BLK, BLK), 1)).astype(F32).astype(BF16)
    rank = jnp.where(mine, dot(ones, upto), 0.0).astype(BF16)
    row = jnp.where(mine, (table & (ROWS - 1)).astype(F32), 0.0).astype(BF16)
    spread = (iota((n * SLOT, 2 * n), 0) >> 3) == (iota((n * SLOT, 2 * n), 1) >> 1)
    spread = spread.astype(F32).astype(BF16)
    rank_all = dot(spread, rank)
    row_all = dot(spread, row)
    slots = ((iota((n * SLOT, BLK), 0) & (SLOT - 1)) + 1).astype(F32)
    picked = jnp.sum(
        jnp.where(rank_all == slots, row_all + 1.0, 0.0), axis=1, keepdims=True
    ) - 1.0
    lane = iota((n * SLOT, ROWS), 1).astype(F32)
    choose = (lane == picked).astype(F32).astype(BF16)
    give_kv[:, :, :HD] = dot(choose, ck_ref[...]).reshape(n, SLOT, HD).astype(BF16)
    give_kv[:, :, HD:] = dot(choose, cv_ref[...]).reshape(n, SLOT, HD).astype(BF16)
    give_q[...] = dot(choose, cq_ref[...]).reshape(n, SLOT, wide).astype(BF16)

    def give(src, dst, out_sem, in_sem, i):
        peer = lax.rem(me + i, n)
        return pltpu.make_async_remote_copy(
            src_ref=src.at[peer],
            dst_ref=dst.at[me],
            send_sem=out_sem.at[i],
            recv_sem=in_sem.at[i],
            device_id={"ctx": peer},
            device_id_type=MESH,
        )

    def given(src, dst, out_sem, in_sem, i):
        peer = lax.rem(me + n - i, n)
        return pltpu.make_async_remote_copy(
            src_ref=src.at[peer],
            dst_ref=dst.at[peer],
            send_sem=out_sem.at[i],
            recv_sem=in_sem.at[i],
            device_id={"ctx": peer},
            device_id_type=MESH,
        )

    kv_rows = (give_kv, take_kv, give_kv_sem, take_kv_sem)
    q_rows = (give_q, take_q, give_q_sem, take_q_sem)

    def each(action):
        def body(i, carry):
            action(i)
            return carry

        lax.fori_loop(1, n, body, 0)

    pl.semaphore_wait(barrier, n - 1 + 2)
    each(lambda i: give(*kv_rows, i).start())
    each(lambda i: give(*q_rows, i).start())
    take_kv[me] = give_kv[me]
    take_q[me] = give_q[me]

    bound = jnp.concatenate(
        [patch_ref[pl.ds(2 * me, 1), :], patch_ref[pl.ds(2 * me + 1, 1), :]], axis=1
    )
    bound = (bound >> 8).astype(F32)
    same = iota((ROWS, ROWS), 0) == iota((ROWS, ROWS), 1)
    origin_col = jnp.sum(jnp.where(same, bound, 0.0), axis=1, keepdims=True)
    before = (origin_col == bound) & (iota((ROWS, ROWS), 1) < iota((ROWS, ROWS), 0))
    place = origin_col * SLOT + jnp.sum(jnp.where(before, 1.0, 0.0), axis=1, keepdims=True)
    replaced = origin_col >= 0.0
    lane = iota((ROWS, n * SLOT), 1).astype(F32)
    settle = ((lane == place) & replaced).astype(F32).astype(BF16)

    def merge(got, base):
        got = got.astype(F32).reshape(n * SLOT, HD).astype(BF16)
        return jnp.where(replaced, dot(settle, got), base.astype(F32)).astype(BF16)

    lens = lens_ref[...].astype(F32)
    docs = lens.shape[1]
    d0, d1 = iota((docs, HD), 0), iota((docs, HD), 1)
    eye = iota((docs, docs), 0) == iota((docs, docs), 1)
    lens_col = jnp.sum(jnp.where(eye, lens, 0.0), axis=1, keepdims=True)
    ends = jnp.sum(jnp.where(d0 <= d1, lens_col, 0.0), axis=0, keepdims=True)
    starts = jnp.sum(jnp.where(d0 < d1, lens_col, 0.0), axis=0, keepdims=True)

    def in_doc(first):
        pos = (first + iota((ROWS, HD), 0)).astype(F32)
        return (pos >= starts) & (pos < ends)

    corner_out = (x + 3 <= last) & (y == SIDE - 1)
    corner_in = (x >= 3) & (y == 0)
    partner = {"ctx": chip * 2 + other}

    def device(to_x, to_y):
        return {"ctx": (to_x * SIDE + to_y) * 2 + core}

    def along(step):
        return lax.rem(y + SIDE + step, SIDE)

    def part(slot, c):
        return kv.at[slot, c, :, :, pl.ds(0, HD)]

    def remote(kind, src, slot, to):
        return pltpu.make_async_remote_copy(
            src_ref=src,
            dst_ref=part(slot, core),
            send_sem=send_sem.at[kind],
            recv_sem=recv_sem.at[kind],
            device_id=to,
            device_id_type=MESH,
        )

    def needs(dx, source, to):
        there = x >= dx
        near = jnp.where(dx == 0, to > source, True)
        far = jnp.where(dx == 2, source >= to - 1, True)
        corner = jnp.where(dx == 3, (to == 0) & (source == SIDE - 1), True)
        return there & near & far & corner

    def held(dx):
        return own if dx == 0 else part(dx * SIDE + y, core)

    def outgoing():
        yield 0, x < last, remote(0, own, SIDE + y, device(x + 1, y))
        yield 1, (x >= 1) & (x < last), remote(
            1, part(SIDE + y, core), 2 * SIDE + y, device(x + 1, y)
        )
        yield 2, corner_out, remote(2, own, 4 * SIDE - 1, device(x + 3, 0))
        for dx in range(3):
            yield 3 + dx, needs(dx, y, along(way)) | needs(dx, y, along(2)), remote(
                3 + dx, held(dx), dx * SIDE + y, device(x, along(way))
            )
            yield 6 + dx, needs(dx, y, along(-way)), remote(
                6 + dx, held(dx), dx * SIDE + y, device(x, along(-way))
            )
            slot = dx * SIDE + along(-way)
            yield 9 + dx, needs(dx, along(-way), along(way)), remote(
                9 + dx, part(slot, core), slot, device(x, along(way))
            )

    sends = {kind: (cond, copy) for kind, cond, copy in outgoing()}

    def arriving():
        yield 0, x >= 1, x >= 1, SIDE + y, device(x - 1, y)
        yield 1, x >= 2, x >= 2, 2 * SIDE + y, device(x - 1, y)
        yield 2, corner_in, corner_in, 4 * SIDE - 1, device(x - 3, SIDE - 1)
        for dx in range(3):
            source = along(-way)
            read = needs(dx, source, y)
            yield 3 + dx, read | needs(dx, source, along(way)), read, dx * SIDE + source, device(
                x, source
            )
            source = along(way)
            read = needs(dx, source, y)
            yield 6 + dx, read, read, dx * SIDE + source, device(x, source)
            source = along(2)
            read = needs(dx, source, y)
            yield 9 + dx, read, read, dx * SIDE + source, device(x, along(-way))

    arrivals = {kind: rest for kind, *rest in arriving()}

    def start(*kinds):
        for kind in kinds:
            cond, copy = sends[kind]

            @pl.when(cond)
            def _(copy=copy):
                copy.start()

    def relay(slot):
        return pltpu.make_async_remote_copy(
            src_ref=part(slot, core),
            dst_ref=part(slot, core),
            send_sem=pass_sem.at[slot],
            recv_sem=got_sem.at[slot],
            device_id=partner,
            device_id_type=MESH,
        )

    def relayed(slot):
        return pltpu.make_async_remote_copy(
            src_ref=part(slot, other),
            dst_ref=part(slot, other),
            send_sem=pass_sem.at[slot],
            recv_sem=got_sem.at[slot],
            device_id=partner,
            device_id_type=MESH,
        )

    def take(kind, *then):
        cond, read, slot, origin = arrivals[kind]

        @pl.when(cond)
        def _():
            remote(kind, own, slot, origin).wait_recv()

        start(*then)

        @pl.when(read)
        def _():
            relay(slot).start()

    own_to_partner = pltpu.make_async_remote_copy(
        src_ref=own,
        dst_ref=part(y, core),
        send_sem=pass_sem.at[y],
        recv_sem=got_sem.at[y],
        device_id=partner,
        device_id_type=MESH,
    )
    each(lambda i: given(*kv_rows, i).wait_recv())
    fresh_k = merge(take_kv[:, :, :HD], k_ref[...])
    fresh_v = merge(take_kv[:, :, HD:], v_ref[...])
    own[0] = fresh_k
    own[1] = fresh_v
    kv[y, core, 0, :, :HD] = fresh_k
    kv[y, core, 1, :, :HD] = fresh_v

    @pl.when(core == 0)
    def _():
        kv[y, 1, :, :, :HD] = jnp.zeros_like(own[...])

    start(0, 3, 6, 2)

    @pl.when(core == 0)
    def _():
        own_to_partner.start()

    def mark(slot):
        dx, source = slot // SIDE, lax.rem(slot, SIDE)
        for c in (0, 1):
            here = in_doc((((x - dx) * SIDE + source) * 2 + c) * ROWS)
            kv[slot, c, 0, :, HD:] = jnp.where(here, 1.0, 0.0).astype(BF16)
            kv[slot, c, 1, :, HD:] = jnp.ones((ROWS, HD), BF16)

    def mark_one(slot, carry):
        mark(slot)
        return carry

    lax.fori_loop(0, 3 * SIDE, mark_one, 0)
    mark(4 * SIDE - 1)

    far = jnp.where(in_doc(me * ROWS), 0.0, FAR).astype(BF16)
    each(lambda i: given(*q_rows, i).wait_recv())
    for h in range(heads):
        lanes = slice(h * HD, (h + 1) * HD)
        rows[h, :, :HD] = merge(take_q[:, :, lanes], q_ref[:, lanes])
        rows[h, :, HD:] = far

    span = 2 * ROWS

    def unit(slot, first):
        keys = kv[slot, :, 0].reshape(span, 2 * HD)
        vals = kv[slot, :, 1].reshape(span, 2 * HD)
        for h in range(heads):
            scores = lax.dot_general(
                rows[h], keys, (((1,), (1,)), ((), ())), preferred_element_type=F32
            )
            if first:
                seen = iota((ROWS, span), 1) <= core * ROWS + iota((ROWS, span), 0)
                scores = jnp.where(seen, scores, 8.0 * FAR)
            new = jnp.max(scores, axis=1, keepdims=True)
            if first:
                new = jnp.broadcast_to(new, (ROWS, HD))
            else:
                old = top[h]
                new = jnp.maximum(old, new)
                scale = jnp.exp2((old - new) * EXP2)
            weights = jnp.concatenate(
                [
                    jnp.exp2((scores[:, t * HD : (t + 1) * HD] - new) * EXP2).astype(BF16)
                    for t in range(span // HD)
                ],
                axis=1,
            )
            mixed = dot(weights, vals)
            top[h] = new
            if first:
                acc[h] = mixed[:, :HD]
                total[h] = mixed[:, HD:]
            else:
                acc[h] = acc[h] * scale + mixed[:, :HD]
                total[h] = total[h] * scale + mixed[:, HD:]

    order = ((1, 0), (0, 1), (0, 3), (2, 0), (1, 1), (1, 3),
             (0, 2), (2, 1), (2, 3), (1, 2), (3, 3), (2, 2))
    code_x = sum(dx << (2 * i) for i, (dx, _) in enumerate(order))
    code_y = sum(dy << (2 * i) for i, (_, dy) in enumerate(order))

    def serve(i):
        if i == 0:
            take(0, 1, 4, 7)
            take(3, 9)
            take(6)
        if i == 3:
            take(1, 5, 8)
        if i == 4:
            take(4, 10)
            take(7)
            take(9)
        if i == 7:
            take(5, 11)
            take(8)
        if i == 9:
            take(10)
            take(2)
        if i == 11:
            take(11)

    serve(0)

    @pl.when(core == 1)
    def _():
        relayed(y).wait_recv()

    unit(y, True)

    def step(i, carry):
        for at in (3, 4, 7, 9, 11):

            @pl.when(i == at)
            def _(at=at):
                serve(at)

        dx = (code_x >> (2 * i)) & 3
        source = lax.rem(y + ((code_y >> (2 * i)) & 3), SIDE)
        slot = dx * SIDE + source

        @pl.when(needs(dx, source, y))
        def _():
            relayed(slot).wait_recv()
            unit(slot, False)

        return carry

    lax.fori_loop(0, len(order), step, 0)

    for h in range(heads):
        mixed_heads[:, h * HD : (h + 1) * HD] = (acc[h] / total[h]).astype(BF16)

    half = groups // 2

    def hops(t):
        return (half, groups - 1 - half) if t % 2 == 0 else (groups - 1 - half, half)

    def move(t, way, s):
        slot = s if way == 0 else hops(t)[0] + s
        return pltpu.make_async_remote_copy(
            src_ref=out_buf.at[t, slot],
            dst_ref=in_buf.at[t, slot],
            send_sem=up_sem.at[t, slot],
            recv_sem=down_sem.at[t, slot],
            device_id={"head": up if way == 0 else down},
            device_id_type=MESH,
        )

    def stage(t, s):
        if s == 0:
            fetch(t).wait()
            part_sum[t] = dot(mixed_heads[...], w[t]).reshape(groups, share, cols)
        result = part_sum[t, group] if s == half else None
        for way in (0, 1):
            length = hops(t)[way]
            base = 0 if way == 0 else hops(t)[0]
            if s < length:
                left = length - s
                to = lax.rem(group + (left if way == 0 else groups - left), groups)
                value = part_sum[t, to]
                if s > 0:
                    move(t, way, s - 1).wait_recv()
                    value = value + in_buf[t, base + s - 1].astype(F32)
                out_buf[t, base + s] = value.astype(BF16)
                move(t, way, s).start()
            if s == half:
                move(t, way, length - 1).wait_recv()
                result = result + in_buf[t, base + length - 1].astype(F32)
        if s == half:
            out_ref[:, t * cols : (t + 1) * cols] = result.astype(BF16)

    for s in range(half + 1):
        for t in range(TILES):
            stage(t, s)
    for t in range(TILES):
        for way in (0, 1):
            for s in range(hops(t)[way]):
                move(t, way, s).wait_send()

    for kind in range(12):
        cond, copy = sends[kind]

        @pl.when(cond)
        def _(copy=copy):
            copy.wait_send()

        _, read, slot, _ = arrivals[kind]

        @pl.when(read)
        def _(slot=slot):
            relay(slot).wait_send()

    @pl.when(core == 0)
    def _():
        own_to_partner.wait_send()
    each(lambda i: give(*kv_rows, i).wait_send())
    each(lambda i: give(*q_rows, i).wait_send())


def per_device(
    queries, keys, values, cf_queries, cf_keys, cf_values, patch_source, doc_lengths, out_weight
):
    ctx = lax.axis_size("ctx")
    groups = lax.axis_size("head")
    wide = queries.shape[1]
    heads = wide // HD
    feats = out_weight.shape[1]
    share, cols = ROWS // groups, feats // TILES
    dma = pltpu.SemaphoreType.DMA
    return pl.pallas_call(
        layer_kernel,
        name="layer",
        out_shape=jax.ShapeDtypeStruct((share, feats), BF16),
        in_specs=[VMEM] * 8 + [ANY],
        out_specs=VMEM,
        scratch_shapes=[
            pltpu.VMEM((ctx, SLOT, 2 * HD), BF16),
            pltpu.VMEM((ctx, SLOT, 2 * HD), BF16),
            pltpu.VMEM((ctx, SLOT, wide), BF16),
            pltpu.VMEM((ctx, SLOT, wide), BF16),
            pltpu.VMEM((2, ROWS, HD), BF16),
            pltpu.VMEM((heads, ROWS, 2 * HD), BF16),
            pltpu.VMEM((4 * SIDE, 2, 2, ROWS, 2 * HD), BF16),
            pltpu.VMEM((heads, ROWS, HD), F32),
            pltpu.VMEM((heads, ROWS, HD), F32),
            pltpu.VMEM((heads, ROWS, HD), F32),
            pltpu.VMEM((ROWS, wide), BF16),
            pltpu.VMEM((TILES, wide, cols), BF16),
            pltpu.VMEM((TILES, groups, share, cols), F32),
            pltpu.VMEM((TILES, groups - 1, share, cols), BF16),
            pltpu.VMEM((TILES, groups - 1, share, cols), BF16),
            dma((ctx,)),
            dma((ctx,)),
            dma((ctx,)),
            dma((ctx,)),
            dma((12,)),
            dma((12,)),
            dma((4 * SIDE,)),
            dma((4 * SIDE,)),
            dma((TILES,)),
            dma((TILES, groups - 1)),
            dma((TILES, groups - 1)),
        ],
        compiler_params=pltpu.CompilerParams(collective_id=0, has_side_effects=True),
    )(
        patch_source.reshape(2 * ctx, BLK), doc_lengths.reshape(1, -1),
        queries, keys, values, cf_queries, cf_keys, cf_values, out_weight,
    )


def solution(mesh):
    in_specs = (
        P("ctx", "head"),
        P("ctx", "head"),
        P("ctx", "head"),
        P("ctx", "head"),
        P("ctx", "head"),
        P("ctx", "head"),
        P(),
        P(),
        P("head", None),
    )
    out_specs = P(("ctx", "head"), None)
    return jax.shard_map(
        per_device, mesh=mesh, in_specs=in_specs, out_specs=out_specs, check_vma=False
    )
```
